768 devices in a mesh: tower: 12 (over z), member: 8 (over y), rep: 8 (over x, core).
Axes of the slice: x: 4, y: 8, z: 12, core: 2. Of those that a mesh axis runs over, the one named last changes fastest.
Arguments:
- pooled: bfloat16 [12, 8, 8, 64, 96, 128], P('tower', 'member', 'rep'), may hold values from -6 to 6
- live_count: int32 [12], P('tower'), may hold values from 1 to 8, as said below
- row_map: int32 [8, 8, 768], P('member', 'rep'), may hold values from 0 to 767, as said below
- tower_in: bfloat16 [12, 1024, 512], P('tower'), may hold values from -0.1875 to 0.1875
- bias_in: float32 [12, 512], P('tower'), may hold values from -3 to 3
- tower_out: bfloat16 [12, 512, 288], P('tower'), may hold values from -0.25 to 0.25
- bias_out: float32 [12, 288], P('tower'), may hold values from -3 to 3
- cross_down: bfloat16 [3456, 512], replicated, may hold values from -0.109375 to 0.109375
- cross_up: bfloat16 [512, 3456], replicated, may hold values from -0.25 to 0.25
- cross_bias: float32 [3456], replicated, may hold values from -3 to 3
- grad_out: bfloat16 [8, 8, 768, 3456], P('member', 'rep', 'tower'), may hold values from -6 to 6
Outputs:
- crossed: bfloat16 [8, 8, 768, 3456], P('member', 'rep', 'tower')
- pooled_grad: bfloat16 [12, 8, 8, 64, 96, 128], P('tower', 'member', 'rep')
The draws below stay inside these ranges and needn't reach their ends.
Inputs may be any that keep to these rules, and one draw needn't show every extreme that they name: Slot k of tower t holds a feature exactly when k < live_count[t]; some tower has 8 live slots and another has 1. `row_map`: for every member and rep index the 768 entries are a permutation of 0 to 767.
All inputs are finite; a program needn't handle non-finite values.
Results may differ from the reference program's by a relative error of at most 0.008.
Values may be sent and summed in bfloat16 or wider, within the bound.
No kernel may reach another device: no remote copies, remote signals or barrier semaphores. Data moves between devices by JAX's collectives and lax.ppermute only.
A program may use at most 64 MiB of HBM per device.

```python
import jax
import jax.numpy as jnp
from jax import lax

EMB = 128
SLOTS = 8
HID = 512
CROSS = 3456
RANK = 512
TOUT = 288
S_DEV = 768
SP = 96
GROUPS = 64
N_TOWER = 12
N_MEMBER = 8
N_REP = 8


def draw_live_count(key, part):
    counts = jax.random.randint(jax.random.fold_in(key, 11), (N_TOWER,), 1, SLOTS + 1)
    fullest = jax.random.randint(jax.random.fold_in(key, 12), (), 0, N_TOWER)
    offset = jax.random.randint(jax.random.fold_in(key, 13), (), 1, N_TOWER)
    emptiest = (fullest + offset) % N_TOWER
    counts = counts.at[fullest].set(SLOTS).at[emptiest].set(1)
    return counts.astype(jnp.int32)


def draw_row_map(key, part):
    keys_all = jax.random.split(jax.random.fold_in(key, 21), GROUPS)
    orders = jax.vmap(lambda single: jax.random.permutation(single, S_DEV))(keys_all)
    return orders.reshape(N_MEMBER, N_REP, S_DEV).astype(jnp.int32)


def level_of(own_key, extent, shards, smallest, top_value):
    gain = 1.0
    for position, blocks in shards:
        steps = jax.random.uniform(jax.random.fold_in(jax.random.fold_in(own_key, 6), position), (blocks,), jnp.float32, smallest / len(shards), top_value / len(shards))
        gain = gain * jnp.repeat(jnp.exp(steps), extent[position] // blocks).reshape((-1,) + (1,) * (len(extent) - 1 - position))
    return gain


def scatter_about(own_key, dims, scale, most, cuts=(), kind=jnp.bfloat16):
    level = level_of(own_key, dims, cuts, -0.22, 0.18) if cuts else 1.0
    result = jax.random.normal(own_key, dims, jnp.float32) * scale * level
    return jnp.minimum(jnp.maximum(result, -most), most).astype(kind)


def setup_inputs(seed: int = 0) -> dict:
    keys = jax.random.split(jax.random.key(seed), 12)
    return {
        "pooled": scatter_about(keys[0], (N_TOWER, SLOTS, N_REP, GROUPS, SP, EMB), 1.0, 6.0, ((0, 12), (1, 8), (2, 8))),
        "live_count": draw_live_count(jax.random.fold_in(keys[11], 71), 0),
        "row_map": draw_row_map(jax.random.fold_in(keys[11], 71), 0),
        "tower_in": scatter_about(keys[3], (N_TOWER, SLOTS * EMB, HID), (SLOTS * EMB) ** -0.5, 0.1875, ((0, 12),)),
        "bias_in": scatter_about(keys[4], (N_TOWER, HID), 0.5, 3.0, ((0, 12),), jnp.float32),
        "tower_out": scatter_about(keys[5], (N_TOWER, HID, TOUT), HID ** -0.5, 0.25, ((0, 12),)),
        "bias_out": scatter_about(keys[6], (N_TOWER, TOUT), 0.5, 3.0, ((0, 12),), jnp.float32),
        "cross_down": scatter_about(keys[7], (CROSS, RANK), CROSS ** -0.5, 0.109375),
        "cross_up": scatter_about(keys[8], (RANK, CROSS), RANK ** -0.5, 0.25),
        "cross_bias": scatter_about(keys[9], (CROSS,), 0.5, 3.0, (), jnp.float32),
        "grad_out": scatter_about(keys[10], (N_MEMBER, N_REP, S_DEV, CROSS), 1.0, 6.0, ((0, 8), (1, 8), (2, 12))),
    }


def silu_slope(preact):
    sigma = jax.nn.sigmoid(preact)
    return sigma * (1.0 + preact * (1.0 - sigma))


def tower_input(pooled_tower, live_tower):
    arranged = jnp.transpose(pooled_tower, (2, 1, 3, 0, 4)).reshape(GROUPS * S_DEV, SLOTS * EMB)
    slot_live = jnp.arange(SLOTS, dtype=jnp.int32) < live_tower
    column_live = jnp.repeat(slot_live, EMB)
    inputs = jnp.where(column_live[None, :], arranged, jnp.zeros((), arranged.dtype))
    return inputs, column_live


def tower_forward(pieces):
    pooled_tower, live_tower, weight_first, bias_first, weight_second, bias_second = pieces
    inputs, column_live = tower_input(pooled_tower, live_tower)
    first_pre = jnp.dot(inputs, weight_first, preferred_element_type=jnp.float32) + bias_first
    hidden = jax.nn.silu(first_pre).astype(jnp.bfloat16)
    second_pre = jnp.dot(hidden, weight_second, preferred_element_type=jnp.float32) + bias_second
    return jax.nn.silu(second_pre).astype(jnp.bfloat16)


def tower_backward(pieces):
    pooled_tower, live_tower, weight_first, bias_first, weight_second, bias_second, out_grad = pieces
    inputs, column_live = tower_input(pooled_tower, live_tower)
    first_pre = jnp.dot(inputs, weight_first, preferred_element_type=jnp.float32) + bias_first
    hidden = jax.nn.silu(first_pre).astype(jnp.bfloat16)
    second_pre = jnp.dot(hidden, weight_second, preferred_element_type=jnp.float32) + bias_second
    second_grad = (out_grad.astype(jnp.float32) * silu_slope(second_pre)).astype(jnp.bfloat16)
    hidden_grad = jnp.dot(second_grad, weight_second.T, preferred_element_type=jnp.float32)
    first_grad = (hidden_grad * silu_slope(first_pre)).astype(jnp.bfloat16)
    input_grad = jnp.dot(first_grad, weight_first.T, preferred_element_type=jnp.float32)
    input_grad = jnp.where(column_live[None, :], input_grad, jnp.zeros((), input_grad.dtype)).astype(jnp.bfloat16)
    return jnp.transpose(input_grad.reshape(GROUPS, N_REP, SP, SLOTS, EMB), (3, 1, 0, 2, 4))


def reference(pooled, live_count, row_map, tower_in, bias_in, tower_out, bias_out, cross_down, cross_up, cross_bias, grad_out):
    results = lax.map(tower_forward, (pooled, live_count, tower_in, bias_in, tower_out, bias_out))
    results = results.reshape(N_TOWER, GROUPS, S_DEV, TOUT)
    mapping = row_map.reshape(GROUPS, S_DEV).astype(jnp.int32)
    group_index = jnp.arange(GROUPS, dtype=jnp.int32)[:, None]
    counting = jnp.broadcast_to(jnp.arange(S_DEV, dtype=jnp.int32)[None, :], (GROUPS, S_DEV))
    inverse = jnp.zeros((GROUPS, S_DEV), jnp.int32).at[group_index, mapping].set(counting)
    permuted = jnp.take_along_axis(results, inverse[None, :, :, None], axis=2)
    joined = jnp.transpose(permuted, (1, 2, 0, 3)).reshape(GROUPS * S_DEV, CROSS)
    latent = jnp.dot(joined, cross_down, preferred_element_type=jnp.float32).astype(jnp.bfloat16)
    update = jnp.dot(latent, cross_up, preferred_element_type=jnp.float32) + cross_bias
    joined_wide = joined.astype(jnp.float32)
    crossed = (joined_wide + joined_wide * update).astype(jnp.bfloat16)
    cotangent = grad_out.reshape(GROUPS * S_DEV, CROSS).astype(jnp.float32)
    scaled = (cotangent * joined_wide).astype(jnp.bfloat16)
    latent_grad = jnp.dot(scaled, cross_up.T, preferred_element_type=jnp.float32).astype(jnp.bfloat16)
    joined_grad = (cotangent * (1.0 + update) + jnp.dot(latent_grad, cross_down.T, preferred_element_type=jnp.float32)).astype(jnp.bfloat16)
    spread = jnp.transpose(joined_grad.reshape(GROUPS, S_DEV, N_TOWER, TOUT), (2, 0, 1, 3))
    out_grad = jnp.take_along_axis(spread, mapping[None, :, :, None], axis=2).reshape(N_TOWER, GROUPS * S_DEV, TOUT)
    pooled_grad = lax.map(tower_backward, (pooled, live_count, tower_in, bias_in, tower_out, bias_out, out_grad))
    return crossed.reshape(N_MEMBER, N_REP, S_DEV, CROSS), pooled_grad
```

```python
import functools

import jax
import jax.numpy as jnp
from jax import lax
from jax.experimental import pallas as pl
from jax.experimental.pallas import tpu as pltpu
from jax.sharding import PartitionSpec as P

BF = jnp.bfloat16
F32 = jnp.float32
LANES = 128
QUAD = 32


def mm(a, b):
    return jnp.dot(a, b, preferred_element_type=F32)


def mm_t(a, b):
    return lax.dot_general(a, b, (((1,), (1,)), ((), ())), preferred_element_type=F32)


def silu(z):
    return z * jax.nn.sigmoid(z)


def silu_slope(z):
    s = jax.nn.sigmoid(z)
    return s * (1.0 + z * (1.0 - s))


def lane_quad(shape):
    return lax.broadcasted_iota(jnp.int32, shape, 1) // QUAD


def prep_body(live_ref, along_ref, down_ref, w1_ref, put_ref, take_ref, w1m_ref):
    rows = put_ref.shape[0]
    put_ref[...] = jnp.where(
        lax.broadcasted_iota(jnp.int32, (rows, rows), 0) == along_ref[...], 1.0, 0.0
    ).astype(BF)
    take_ref[...] = jnp.where(
        lax.broadcasted_iota(jnp.int32, (rows, rows), 1) == down_ref[...], 1.0, 0.0
    ).astype(BF)
    for k in range(w1_ref.shape[0] // LANES):
        rs = slice(k * LANES, (k + 1) * LANES)

        @pl.when(k < live_ref[0])
        def _():
            w1m_ref[rs, :] = w1_ref[rs, :]

        @pl.when(k >= live_ref[0])
        def _():
            w1m_ref[rs, :] = jnp.zeros((LANES, w1_ref.shape[1]), BF)


def forward_body(x_ref, w1_ref, b1_ref, w2_ref, b2_ref, put_ref, out_ref, fp_ref, sp_ref, tr_ref, *, step):
    slots, rows, _ = x_ref.shape
    peers = out_ref.shape[0]
    own = rows // peers
    quarter = own // 4
    for c in range(rows // step):
        rs = slice(c * step, (c + 1) * step)
        x = jnp.concatenate([x_ref[k, rs, :] for k in range(slots)], axis=1)
        fp = mm(x, w1_ref[...]) + b1_ref[...]
        fp_ref[rs, :] = fp
        sp = mm(silu(fp).astype(BF), w2_ref[...]) + b2_ref[...]
        sp_ref[rs, :] = sp
        tr_ref[rs, :] = silu(sp).astype(BF)
    quad = lane_quad((quarter, LANES))
    for c in range(rows // step):
        moved = mm(put_ref[c * step : (c + 1) * step, :], tr_ref[...])
        for s in range(step // own):
            z = c * (step // own) + s
            mine = moved[s * own : (s + 1) * own, :]
            out_ref[z, 0:own, :] = mine[:, 0:LANES].astype(BF)
            out_ref[z, own : 2 * own, :] = mine[:, LANES : 2 * LANES].astype(BF)
            last = mine[:, 2 * LANES :]
            tail = last[0:quarter]
            for j in range(1, 4):
                tail = jnp.where(quad == j, last[j * quarter : (j + 1) * quarter], tail)
            out_ref[z, 2 * own :, :] = tail.astype(BF)


def backward_body(g_ref, take_ref, fp_ref, sp_ref, w1_ref, w2_ref, out_ref, wide_ref, *, step):
    peers = g_ref.shape[0]
    slots, rows, _ = out_ref.shape
    own = rows // peers
    quarter = own // 4
    quad = lane_quad((quarter, LANES))
    for z in range(peers):
        r0 = z * own
        wide_ref[r0 : r0 + own, 0:LANES] = g_ref[z, 0:own, :]
        wide_ref[r0 : r0 + own, LANES : 2 * LANES] = g_ref[z, own : 2 * own, :]
        tail = g_ref[z, 2 * own :, :].astype(F32)
        for j in range(4):
            wide_ref[r0 + j * quarter : r0 + (j + 1) * quarter, 2 * LANES :] = jnp.where(
                quad == j, tail, 0.0
            ).astype(BF)
    for c in range(rows // step):
        rs = slice(c * step, (c + 1) * step)
        og = mm(take_ref[rs, :], wide_ref[...])
        sg = (og * silu_slope(sp_ref[rs, :])).astype(BF)
        hg = mm_t(sg, w2_ref[...])
        fg = (hg * silu_slope(fp_ref[rs, :])).astype(BF)
        ig = mm_t(fg, w1_ref[...])
        for k in range(slots):
            out_ref[k, rs, :] = ig[:, k * LANES : (k + 1) * LANES].astype(BF)


def rolled(v, shift):
    shift %= LANES
    return pltpu.roll(v, shift, 1) if shift else v


def cross_body(j_ref, v_hbm, u_hbm, bias_ref, g_ref, out_ref, crossed_ref,
               v_ref, u_ref, jn_ref, sc_ref, base_ref, jg_ref, sems, *, width, step):
    towers, _, _ = j_ref.shape
    own, total = g_ref.shape
    quarter = own // 4
    get_v = pltpu.make_async_copy(v_hbm, v_ref, sems.at[0])
    get_u = pltpu.make_async_copy(u_hbm, u_ref, sems.at[1])
    get_v.start()
    get_u.start()
    lane = lax.broadcasted_iota(jnp.int32, (own, LANES), 1)
    tiles = [None] * (total // LANES)

    def put(tile, low, high, value):
        held = tiles[tile]
        tiles[tile] = value if held is None else jnp.where((lane >= low) & (lane < high), value, held)

    for t in range(towers):
        first = t * width
        shift = first % LANES
        for h in range(2):
            value = rolled(j_ref[t, h * own : (h + 1) * own, :].astype(F32), shift)
            tile = (first + h * LANES) // LANES
            put(tile, shift, LANES, value)
            if shift:
                put(tile + 1, 0, shift, value)
        start = first + 2 * LANES
        low = start % LANES
        tail = j_ref[t, 2 * own :, :].astype(F32)
        value = jnp.concatenate([rolled(tail, low - j * QUAD) for j in range(4)], axis=0)
        put(start // LANES, low, low + QUAD, value)
    for i, tile in enumerate(tiles):
        cs = slice(i * LANES, (i + 1) * LANES)
        jn_ref[:, cs] = tile.astype(BF)
        sc_ref[:, cs] = (g_ref[:, cs].astype(F32) * tile).astype(BF)
    get_v.wait()
    latent = mm(jn_ref[...], v_ref[...]).astype(BF)
    get_u.wait()
    latent_grad = mm_t(sc_ref[...], u_ref[...]).astype(BF)
    for c in range(total // step):
        cs = slice(c * step, (c + 1) * step)
        update = mm(latent, u_ref[:, cs]) + bias_ref[:, cs]
        j = jn_ref[:, cs].astype(F32)
        crossed_ref[:, cs] = (j + j * update).astype(BF)
        jg_ref[:, cs] = g_ref[:, cs].astype(F32) * (1.0 + update) + mm_t(latent_grad, v_ref[cs, :])
    short = lane_quad((quarter, LANES))
    for t in range(towers):
        first = t * width
        shift = first % LANES
        for h in range(2):
            at = (first + h * LANES) // LANES * LANES
            value = jg_ref[:, at : at + LANES]
            if shift:
                value = jnp.where(lane >= shift, value, jg_ref[:, at + LANES : at + 2 * LANES])
            out_ref[t, h * own : (h + 1) * own, :] = rolled(value, -shift).astype(BF)
        start = first + 2 * LANES
        low = start % LANES
        at = start - low
        tail = None
        for j in range(4):
            value = rolled(jg_ref[j * quarter : (j + 1) * quarter, at : at + LANES], j * QUAD - low)
            tail = value if tail is None else jnp.where(short == j, value, tail)
        out_ref[t, 2 * own :, :] = tail.astype(BF)


def vmem(n):
    return [pl.BlockSpec(memory_space=pltpu.VMEM)] * n


def on_device(pooled, live_count, row_map, tower_in, bias_in, tower_out, bias_out,
              cross_down, cross_up, cross_bias, grad_out):
    groups, piece, emb = pooled.shape[3:]
    slots = lax.axis_size("member")
    reps = lax.axis_size("rep")
    towers = lax.axis_size("tower")
    rows = piece * reps
    own = rows // towers
    hid, width = tower_out.shape[1:]
    rank, total = cross_up.shape
    step = 256 if rows % 256 == 0 else own
    packed = jax.ShapeDtypeStruct((towers, own * width // LANES, LANES), BF)

    received = lax.all_to_all(
        pooled.reshape(groups, piece, emb), ("member", "rep"), split_axis=0, concat_axis=0, tiled=True
    )
    x = received.reshape(slots, rows, emb)

    order = row_map.reshape(rows)
    w1 = tower_in[0]
    put, take, w1m = pl.pallas_call(
        prep_body,
        out_shape=(
            jax.ShapeDtypeStruct((rows, rows), BF),
            jax.ShapeDtypeStruct((rows, rows), BF),
            jax.ShapeDtypeStruct(w1.shape, BF),
        ),
        in_specs=[pl.BlockSpec(memory_space=pltpu.SMEM)] + vmem(3),
        out_specs=tuple(vmem(3)),
        name="prep",
    )(live_count, order.reshape(1, rows), order.reshape(rows, 1), w1)

    def quads(a):
        return jnp.concatenate([a[:, : 2 * LANES]] + [a[:, 2 * LANES :]] * 4, axis=1)

    w2 = quads(tower_out[0])
    b2 = quads(bias_out)
    sent, fp, sp = pl.pallas_call(
        functools.partial(forward_body, step=step),
        out_shape=(
            packed,
            jax.ShapeDtypeStruct((rows, hid), F32),
            jax.ShapeDtypeStruct((rows, 3 * LANES), F32),
        ),
        in_specs=vmem(6),
        out_specs=tuple(vmem(3)),
        scratch_shapes=[pltpu.VMEM((rows, 3 * LANES), BF)],
        name="tower_forward",
    )(x, w1m, bias_in, w2, b2, put)
    joined = lax.all_to_all(sent, "tower", split_axis=0, concat_axis=0, tiled=True)
    joined_grad, crossed = pl.pallas_call(
        functools.partial(cross_body, width=width, step=3 * LANES),
        out_shape=(packed, jax.ShapeDtypeStruct((own, total), BF)),
        in_specs=vmem(1) + [pl.BlockSpec(memory_space=pl.ANY)] * 2 + vmem(2),
        out_specs=tuple(vmem(2)),
        scratch_shapes=[
            pltpu.VMEM((total, rank), BF),
            pltpu.VMEM((rank, total), BF),
            pltpu.VMEM((own, total), BF),
            pltpu.VMEM((own, total), BF),
            pltpu.VMEM((own, total), F32),
            pltpu.VMEM((own, total), F32),
            pltpu.SemaphoreType.DMA((2,)),
        ],
        name="cross",
    )(joined, cross_down, cross_up, cross_bias.reshape(1, total), grad_out.reshape(own, total))
    returned = lax.all_to_all(joined_grad, "tower", split_axis=0, concat_axis=0, tiled=True)
    outgoing = pl.pallas_call(
        functools.partial(backward_body, step=step),
        out_shape=jax.ShapeDtypeStruct((slots, rows, emb), BF),
        in_specs=vmem(6),
        out_specs=vmem(1)[0],
        scratch_shapes=[pltpu.VMEM((rows, 3 * LANES), BF)],
        name="tower_backward",
    )(returned, take, fp, sp, w1m, w2)
    pooled_grad = lax.all_to_all(
        outgoing.reshape(groups, piece, emb), ("member", "rep"), split_axis=0, concat_axis=0, tiled=True
    )
    return (crossed.reshape(grad_out.shape), pooled_grad.reshape(pooled.shape))


def solution(mesh):
    in_specs = (
        P("tower", "member", "rep", None, None, None),
        P("tower"),
        P("member", "rep", None),
        P("tower", None, None),
        P("tower", None),
        P("tower", None, None),
        P("tower", None),
        P(),
        P(),
        P(),
        P("member", "rep", "tower", None),
    )
    out_specs = (P("member", "rep", "tower", None), P("tower", "member", "rep", None, None, None))
    return jax.shard_map(
        on_device, mesh=mesh, in_specs=in_specs, out_specs=out_specs, check_vma=False
    )
```
